512 devices in a mesh: dp: 8 (over x, z_lo), fsdp: 64 (over z_hi, y, core).
Axes of the slice: x: 4, y: 8, z: 8 (z_hi: 4, z_lo: 2; z = z_hi * 2 + z_lo), core: 2. Of those that a mesh axis runs over, the one named last changes fastest.
Arguments:
- tokens: bfloat16 [512, 256, 3584], P(('dp', 'fsdp')), may hold values from -11 to 11
- queries: bfloat16 [512, 256, 1792], P(('dp', 'fsdp')), may hold values from -48 to 48
- key_weight: bfloat16 [3584, 256], P('fsdp'), may hold values from -0.09375 to 0.09375
- value_weight: bfloat16 [3584, 256], P('fsdp'), may hold values from -0.09375 to 0.09375
- key_variance: float32 [3584, 256], P('fsdp'), may hold values from 0.00069754466 to 0.013950893
- sign_bits: int32 [3584, 35], P('fsdp'), may hold values from 0 to 1073741823
Outputs:
- attended: bfloat16 [512, 256, 1792], P(('dp', 'fsdp'))
- spread: bfloat16 [512, 256, 1792], P(('dp', 'fsdp'))
- head_mean: float32 [14], replicated
The draws below stay inside these ranges and needn't reach their ends.
All inputs are finite; a program needn't handle non-finite values.
Results may differ from the reference program's by a relative error of at most 0.014.
The reference program's roundings to bfloat16 on the way (of `tangent`) count: a program that leaves them out, or rounds other values in their place, can miss the bound.
Values may be sent and summed in bfloat16 or wider, within the bound.
A program may use at most 128 MiB of HBM per device.

```python
import math
import jax
import jax.numpy as jnp
import numpy as np
from jax import lax

D = 3584
HD = 128
KVH = 2
QPK = 7
TANG = 4
LEN = 256
HEADS = 14
KVW = 256
WORDS = 35
SEQS = 512


def draw_tokens(key, part):
    base = jnp.clip(jax.random.normal(key, (SEQS, LEN, D), jnp.float32), -6.0, 6.0)
    order = jnp.arange(SEQS, dtype=jnp.float32) / max(SEQS - 1, 1)
    growth = 3.0 ** (0.25 * order)
    return (base * growth[:, None, None]).astype(jnp.bfloat16)


def draw_queries(key, part):
    base = jnp.clip(jax.random.normal(key, (SEQS, LEN, HEADS, HD), jnp.float32), -6.0, 6.0)
    return base.reshape(SEQS, LEN, HEADS * HD).astype(jnp.bfloat16)


def touch_ends(entries, own_key, low, largest):
    longest = entries.shape.index(max(entries.shape))
    spots = []
    for shift in (0, 1):
        where = [jax.random.randint(jax.random.fold_in(own_key, axis), (), 0, length) for axis, length in enumerate(entries.shape)]
        where[longest] = (where[longest] + shift) % entries.shape[longest]
        spots.append(tuple(where))
    return entries.at[spots[0]].set(low).at[spots[1]].set(largest)


def block_levels(stream_key, extent, split, least, largest):
    loudness = 1.0
    for dim, blocks in split:
        heights = jax.random.uniform(jax.random.fold_in(jax.random.fold_in(stream_key, 6), dim), (blocks,), jnp.float32, least / len(split), largest / len(split))
        loudness = loudness * jnp.repeat(jnp.exp(heights), extent[dim] // blocks).reshape((-1,) + (1,) * (len(extent) - 1 - dim))
    return loudness


def scatter_about(stream_key, shape, scale, reach, split=(), held_as=jnp.bfloat16):
    array = scale * jax.random.normal(stream_key, shape, jnp.float32)
    if split:
        array = array * block_levels(stream_key, shape, split, -0.22, 0.18)
    return jnp.clip(array, -reach, reach).astype(held_as)


def setup_inputs(seed: int = 0) -> dict:
    key_of = jax.random.split(jax.random.key(seed), 7)
    return {
        "tokens": draw_tokens(jax.random.fold_in(key_of[6], 71), 0),
        "queries": draw_queries(jax.random.fold_in(key_of[6], 71), 0),
        "key_weight": scatter_about(key_of[2], (D, KVW), D ** -0.5, 0.09375, ((0, 64),)),
        "value_weight": scatter_about(key_of[3], (D, KVW), D ** -0.5, 0.09375, ((0, 64),)),
        "key_variance": jnp.clip(jnp.exp(math.log(0.013950893) - 2.9957322 * jax.random.uniform(key_of[4], (D, KVW), jnp.float32) ** block_levels(key_of[4], (D, KVW), ((0, 64),), -0.2, 0.2)), 0.00069754466, 0.013950893),
        "sign_bits": touch_ends(jax.random.randint(key_of[5], (D, WORDS), 0, 1073741824), jax.random.fold_in(key_of[5], 1), 0, 1073741823).astype(jnp.int32),
    }


word_bits = 30

def sign_table(packed, columns):
    position = np.arange(columns)
    chosen = jnp.take(packed, jnp.asarray(position // word_bits, jnp.int32), axis=1)
    shifted = jnp.right_shift(chosen, jnp.asarray(position % word_bits, jnp.int32))
    return (2 * jnp.bitwise_and(shifted, 1) - 1).astype(jnp.float32)

def make_tangent(key_variance, sign_bits):
    root = jnp.sqrt(key_variance).astype(jnp.bfloat16)
    tiled = jnp.tile(root, (1, TANG)).astype(jnp.float32)
    return (tiled * sign_table(sign_bits, TANG * KVH * HD)).astype(jnp.bfloat16)

def attend(query_rows, key_rows, value_rows, tangent_keys):
    length = query_rows.shape[0]
    factor = HD ** (-0.5)
    causal = jnp.arange(length)[:, None] >= jnp.arange(length)[None, :]
    outputs = []
    spreads = []
    tangent_split = tangent_keys.reshape(length, TANG, KVH, HD)
    for group in range(KVH):
        query_group = query_rows[:, group * QPK * HD:(group + 1) * QPK * HD].reshape(length, QPK, HD).astype(jnp.float32)
        key_group = key_rows[:, group * HD:(group + 1) * HD].astype(jnp.float32)
        value_group = value_rows[:, group * HD:(group + 1) * HD].astype(jnp.float32)
        tangent_group = tangent_split[:, :, group, :].astype(jnp.float32)
        scores = jnp.einsum('qhd,kd->hqk', query_group, key_group) * factor
        scores = jnp.where(causal, scores, -jnp.inf)
        raised = jnp.exp(scores - lax.optimization_barrier(jnp.max(scores, axis=-1, keepdims=True)))
        weights = raised / lax.optimization_barrier(jnp.sum(raised, axis=-1, keepdims=True))
        rounded = weights.astype(jnp.bfloat16).astype(jnp.float32)
        outputs.append(jnp.einsum('hqk,kd->qhd', rounded, value_group).reshape(length, QPK * HD))
        moved = jnp.einsum('qhd,ktd->thqk', query_group, tangent_group) * factor
        centred = weights * (moved - lax.optimization_barrier(jnp.sum(weights * moved, axis=-1, keepdims=True)))
        centred_rounded = centred.astype(jnp.bfloat16).astype(jnp.float32)
        response = jnp.einsum('thqk,kd->tqhd', centred_rounded, value_group)
        spreads.append((lax.optimization_barrier(jnp.sum(response * response, axis=0)) / TANG).reshape(length, QPK * HD))
    return (jnp.concatenate(outputs, axis=1), jnp.concatenate(spreads, axis=1))

def reference(tokens, queries, key_weight, value_weight, key_variance, sign_bits):
    tangent = make_tangent(key_variance, sign_bits)

    def one_sequence(pair):
        token_rows, query_rows = pair
        key_rows = jnp.dot(token_rows, key_weight, preferred_element_type=jnp.float32).astype(jnp.bfloat16)
        value_rows = jnp.dot(token_rows, value_weight, preferred_element_type=jnp.float32).astype(jnp.bfloat16)
        tangent_keys = jnp.dot(token_rows, tangent, preferred_element_type=jnp.float32).astype(jnp.bfloat16)
        attended, variance = attend(query_rows, key_rows, value_rows, tangent_keys)
        head_sums = lax.optimization_barrier(jnp.sum(variance.reshape(-1, HEADS, HD), axis=(0, 2)))
        return (attended.astype(jnp.bfloat16), variance.astype(jnp.bfloat16), head_sums)
    attended, spread, head_sums = lax.map(one_sequence, (tokens, queries))
    head_mean = lax.optimization_barrier(jnp.sum(head_sums, axis=0)) / (SEQS * LEN * HD)
    return (attended, spread, head_mean)
```

```python
import functools

import jax
import jax.numpy as jnp
from jax import lax
from jax.experimental import pallas as pl
from jax.experimental.pallas import tpu as pltpu
from jax.sharding import Mesh
from jax.sharding import PartitionSpec as P

HD = 128
KVH = 2
QPK = 7
TANG = 4
HEADS = KVH * QPK
LEN = 256
D = 3584
KVW = KVH * HD
HALF = 3 * HD
WORD_BITS = 30
WORDS = 35
SHARD = 56
WROWS = 24
WLANES = 40
MESH = pl.DeviceIdType.MESH
FSDP = ("fsdp_0", "fsdp_1", "fsdp_2")
ALL = ("dp_0", "dp_1", "fsdp_0", "fsdp_1", "fsdp_2")

SPLIT = ((0, -1), (-2, 1), (2, -3), (4, 3))


def gather_kernel(
    key_ref, value_ref, var_ref, bits_ref,
    buf_a, buf_b, buf_w,
    own_a, own_b, own_w, wide,
    send_a, send_b, send_w, recv_a, recv_b, recv_w, sib_a, sib_b, sib_w, local,
):
    zl = lax.axis_index("dp_1")
    zh = lax.axis_index("fsdp_0")
    y = lax.axis_index("fsdp_1")
    c = lax.axis_index("fsdp_2")
    side = 2 * zl - 1
    g1 = lax.rem(zh + side + 4, 4)
    g2 = lax.rem(zh - side + 4, 4)
    g3 = lax.rem(zh + 2, 4)
    up = {"fsdp_1": lax.rem(y + 1, 8)}
    down = {"fsdp_1": lax.rem(y + 7, 8)}
    near = {"dp_1": 1 - zl, "fsdp_0": g1}
    far = {"dp_1": 1 - zl}
    twin = {"fsdp_2": 1 - c}
    barrier = pltpu.get_barrier_semaphore()
    for peer in (up, down, near, far, twin):
        pl.semaphore_signal(barrier, inc=1, device_id=peer, device_id_type=MESH)

    own_a[:, :KVW] = jnp.sqrt(var_ref[...]).astype(jnp.bfloat16)
    own_a[:, KVW:] = key_ref[:, :HD]
    own_b[:, :HD] = key_ref[:, HD:]
    own_b[:, HD:] = value_ref[...]
    wide[...] = jnp.zeros_like(wide)
    wide[:, :WORDS] = bits_ref[...]
    spread = wide[0:24, :] + pltpu.roll(wide[24:48, :], WLANES, 1)
    own_w[...] = spread
    own_w[0:8, :] = spread[0:8, :] + pltpu.roll(wide[48:56, :], 2 * WLANES, 1)
    pl.semaphore_wait(barrier, 5)

    kinds = {
        "a": (buf_a, own_a, SHARD, send_a, recv_a, sib_a),
        "b": (buf_b, own_b, SHARD, send_b, recv_b, sib_b),
        "w": (buf_w, own_w, WROWS, send_w, recv_w, sib_w),
    }
    sent = []

    def place(kind, group, row, core):
        buf, _, size, _, _, _ = kinds[kind]
        start = pl.multiple_of((group * 16 + row * 2 + core) * size, 8)
        return buf.at[pl.ds(start, size), :]

    def push(kind, group, row, way, peer, own=False):
        _, mine, _, send, recv, sib = kinds[kind]
        slot = group * 8 + row
        there = place(kind, group, row, c)
        copy = pltpu.make_async_remote_copy(
            src_ref=mine if own else there,
            dst_ref=there,
            send_sem=send.at[way, slot],
            recv_sem=(sib if way == 3 else recv).at[slot],
            device_id=peer,
            device_id_type=MESH,
        )
        copy.start()
        sent.append(copy)

    def arrive(kind, group, row):
        _, _, _, send, recv, _ = kinds[kind]
        slot = group * 8 + row
        there = place(kind, group, row, c)
        pltpu.make_async_remote_copy(
            src_ref=there, dst_ref=there, send_sem=send.at[0, slot], recv_sem=recv.at[slot],
            device_id=twin, device_id_type=MESH,
        ).wait_recv()

    def at(offset):
        return lax.rem(y + offset + 8, 8)

    UP, DOWN, ZED, SIB = 0, 1, 2, 3
    for kind in ("a", "w", "b"):
        push(kind, zh, y, UP, up, True)
        push(kind, zh, y, DOWN, down, True)
        push(kind, zh, y, ZED, near, True)
    for kind in ("a", "w", "b"):
        push(kind, zh, y, SIB, twin, True)
    locals_ = []
    for i, kind in enumerate(("a", "b", "w")):
        copy = pltpu.make_async_copy(kinds[kind][1], place(kind, zh, y, c), local.at[i])
        copy.start()
        locals_.append(copy)

    reach = {0: (4, 3), 1: (3, 4), 2: (4, 3), 3: (3, 4)}
    groups = (zh, g1, g2, g3)
    low = lax.rem(y + zl, 2)

    def pick(pair, which):
        return pair[0] * (1 - which) + pair[1] * which

    for r in range(1, 9):
        if r <= 3:
            arrive("b", groups[r], y)
            if r == 1:
                push("b", g1, y, ZED, far)
            if r == 2:
                push("b", g2, y, ZED, near)
            push("b", groups[r], y, UP, up)
            push("b", groups[r], y, DOWN, down)
            push("b", groups[r], y, SIB, twin)
        for d, way, peer, limit, sign in ((r, UP, up, 4, -1), (r, DOWN, down, 3, 1)):
            if d <= limit:
                for kind in ("a", "w"):
                    row = at(sign * d)
                    arrive(kind, zh, row)
                    if d < limit:
                        push(kind, zh, row, way, peer)
                    push(kind, zh, row, ZED, near)
                    push(kind, zh, row, SIB, twin)
        for delay in range(4):
            d = r - delay
            if d < 1:
                continue
            for way, peer, limit, sign in ((UP, up, reach[delay][0], -1), (DOWN, down, reach[delay][1], 1)):
                if d <= limit:
                    row = at(sign * d)
                    arrive("b", groups[delay], row)
                    if d < limit:
                        push("b", groups[delay], row, way, peer)
                    push("b", groups[delay], row, SIB, twin)
        d = r - 1
        if d <= 4:
            for offset in ((0,) if d == 0 else (-4,) if d == 4 else (-d, d)):
                for kind in ("a", "w"):
                    arrive(kind, g1, at(offset))
                    push(kind, g1, at(offset), ZED, far)
                    push(kind, g1, at(offset), SIB, twin)
        if r in (4, 6):
            for pair in SPLIT[r - 4 : r - 2]:
                for onward in (True, False):
                    row = at(pick(pair, 1 - low if onward else low))
                    for kind in ("a", "w"):
                        arrive(kind, g2, row)
                        if onward:
                            push(kind, g2, row, ZED, near)
                        push(kind, g2, row, SIB, twin)
        if r in (5, 7):
            for pair in SPLIT[r - 5 : r - 3]:
                row = at(pick(pair, low))
                for kind in ("a", "w"):
                    arrive(kind, g3, row)
                    push(kind, g3, row, ZED, far)
                    push(kind, g3, row, SIB, twin)
        if r in (6, 8):
            for pair in SPLIT[r - 6 : r - 4]:
                row = at(pick(pair, 1 - low))
                for kind in ("a", "w"):
                    arrive(kind, g3, row)
                    push(kind, g3, row, SIB, twin)

    for copy in locals_:
        copy.wait()

    def last(slot, _):
        group, row = slot // 8, lax.rem(slot, 8)
        for kind in ("a", "b", "w"):
            _, _, _, send, _, sib = kinds[kind]
            there = place(kind, group, row, 1 - c)
            pltpu.make_async_remote_copy(
                src_ref=there, dst_ref=there, send_sem=send.at[0, slot], recv_sem=sib.at[slot],
                device_id=twin, device_id_type=MESH,
            ).wait_recv()
        return 0

    lax.fori_loop(0, 32, last, 0)
    for copy in sent:
        copy.wait_send()


def gather(key_weight, value_weight, key_variance, sign_bits):
    vmem = pl.BlockSpec(memory_space=pltpu.VMEM)
    return pl.pallas_call(
        gather_kernel,
        out_shape=(
            jax.ShapeDtypeStruct((D, HALF), jnp.bfloat16),
            jax.ShapeDtypeStruct((D, HALF), jnp.bfloat16),
            jax.ShapeDtypeStruct((64 * WROWS, HD), jnp.int32),
        ),
        in_specs=[vmem] * 4,
        out_specs=(vmem,) * 3,
        scratch_shapes=[
            pltpu.VMEM((SHARD, HALF), jnp.bfloat16),
            pltpu.VMEM((SHARD, HALF), jnp.bfloat16),
            pltpu.VMEM((WROWS, HD), jnp.int32),
            pltpu.VMEM((SHARD, HD), jnp.int32),
        ]
        + [pltpu.SemaphoreType.DMA((4, 32))] * 3
        + [pltpu.SemaphoreType.DMA((32,))] * 6
        + [pltpu.SemaphoreType.DMA((3,))],
        compiler_params=pltpu.CompilerParams(collective_id=0, has_side_effects=True),
        name="gather",
    )(key_weight, value_weight, key_variance, sign_bits)


def attend_kernel(
    tok_ref, query_ref, buf_a, buf_b, buf_w,
    att_ref, spread_ref, sums_ref,
    tangent, rows,
):
    lane = lax.broadcasted_iota(jnp.int32, (8, HD), 1)
    index, mask = [], []
    for k in range(8):
        column = lane + k * HD
        word = (column * 2185) >> 16
        index.append(word)
        mask.append(jnp.left_shift(jnp.ones_like(column), column - word * WORD_BITS))

    def expand(j, _):
        start = pl.multiple_of(j * 2 * SHARD, 16)
        root = buf_a[pl.ds(start, 2 * SHARD), :KVW].astype(jnp.float32)
        minus = -root
        words = buf_w[pl.ds(pl.multiple_of(j * 2 * WROWS, 8), 2 * WROWS), :]
        for k in range(8):
            cols = slice((k % 2) * HD, (k % 2 + 1) * HD)
            tiles = []
            for core in range(2):
                for rt in range(7):
                    word_tile = words[core * WROWS + (rt % 3) * 8 : core * WROWS + (rt % 3) * 8 + 8]
                    found = jnp.take_along_axis(
                        word_tile, index[k] + WLANES * (rt // 3), axis=1, mode="promise_in_bounds"
                    )
                    at = core * SHARD + rt * 8
                    tiles.append(
                        jnp.where(
                            (found & mask[k]) != 0, root[at : at + 8, cols], minus[at : at + 8, cols]
                        )
                    )
            tangent[pl.ds(start, 2 * SHARD), k * HD : (k + 1) * HD] = jnp.concatenate(
                tiles, axis=0
            ).astype(jnp.bfloat16)
        return 0

    lax.fori_loop(0, 32, expand, 0)
    keys = jnp.concatenate([buf_a[:, KVW:], buf_b[:, :HD]], axis=1)
    rows[:, :KVW] = jnp.dot(tok_ref[...], keys, preferred_element_type=jnp.float32).astype(jnp.bfloat16)
    rows[:, KVW : 2 * KVW] = jnp.dot(
        tok_ref[...], buf_b[:, HD:], preferred_element_type=jnp.float32
    ).astype(jnp.bfloat16)

    def project(t, _):
        cols = pl.ds(pl.multiple_of(t * KVW, KVW), KVW)
        out = pl.ds(pl.multiple_of(2 * KVW + t * KVW, KVW), KVW)
        rows[:, out] = jnp.dot(
            tok_ref[...], tangent[:, cols], preferred_element_type=jnp.float32
        ).astype(jnp.bfloat16)
        return 0

    lax.fori_loop(0, TANG, project, 0)
    attention(query_ref, rows, att_ref, spread_ref, sums_ref)


def attention(query_ref, rows, att_ref, spread_ref, sums_ref):
    factor = HD**-0.5
    causal = lax.broadcasted_iota(jnp.int32, (HD, HD), 0) >= lax.broadcasted_iota(jnp.int32, (HD, HD), 1)
    zeros = jnp.zeros((HD, HD), jnp.bfloat16)
    nt = (((1,), (1,)), ((), ()))

    def spread_out(top, bottom):
        top = jnp.concatenate([top.astype(jnp.bfloat16), zeros], axis=1)
        return jnp.concatenate([top, bottom.astype(jnp.bfloat16)], axis=0)

    def head(h, _):
        g = h // QPK
        cols = pl.ds(pl.multiple_of(h * HD, HD), HD)
        q = query_ref[:, cols]
        key = rows[:, pl.ds(pl.multiple_of(g * HD, HD), HD)]
        value = rows[:, pl.ds(pl.multiple_of(KVW + g * HD, HD), HD)]
        s = lax.dot_general(q, key, nt, preferred_element_type=jnp.float32)

        def soften(x):
            e = jnp.exp((x - jnp.max(x, axis=1, keepdims=True)) * factor)
            return e * (1.0 / jnp.sum(e, axis=1, keepdims=True))

        w0 = soften(jnp.where(causal, s[:HD, :HD], -jnp.inf))
        w1 = soften(
            jnp.concatenate([s[HD:, :HD], jnp.where(causal, s[HD:, HD:], -jnp.inf)], axis=1)
        )
        att_ref[:, cols] = jnp.dot(
            spread_out(w0, w1), value, preferred_element_type=jnp.float32
        ).astype(jnp.bfloat16)
        f0, f1 = w0 * factor, w1 * factor
        total = None
        for t in range(TANG):
            tk = rows[:, pl.ds(pl.multiple_of((2 + t) * KVW + g * HD, HD), HD)]
            m = lax.dot_general(q, tk, nt, preferred_element_type=jnp.float32)
            m0, m1 = m[:HD, :HD], m[HD:, :]
            c0 = f0 * (m0 - jnp.sum(w0 * m0, axis=1, keepdims=True))
            c1 = f1 * (m1 - jnp.sum(w1 * m1, axis=1, keepdims=True))
            resp = jnp.dot(spread_out(c0, c1), value, preferred_element_type=jnp.float32)
            total = resp * resp if total is None else total + resp * resp
        variance = total * (1.0 / TANG)
        spread_ref[:, cols] = variance.astype(jnp.bfloat16)
        sums_ref[h] = jnp.sum(variance.reshape(LEN // 8, 8, HD), axis=0)
        return 0

    lax.fori_loop(0, HEADS, head, 0)


def attend(tokens, queries, buf_a, buf_b, buf_w):
    vmem = pl.BlockSpec(memory_space=pltpu.VMEM)
    return pl.pallas_call(
        attend_kernel,
        out_shape=(
            jax.ShapeDtypeStruct((LEN, HEADS * HD), jnp.bfloat16),
            jax.ShapeDtypeStruct((LEN, HEADS * HD), jnp.bfloat16),
            jax.ShapeDtypeStruct((HEADS, 8, HD), jnp.float32),
        ),
        in_specs=[vmem] * 5,
        out_specs=(vmem,) * 3,
        scratch_shapes=[
            pltpu.VMEM((D, TANG * KVW), jnp.bfloat16),
            pltpu.VMEM((LEN, (2 + TANG) * KVW), jnp.bfloat16),
        ],
        compiler_params=pltpu.CompilerParams(vmem_limit_bytes=56 * 1024 * 1024),
        name="attend",
    )(tokens, queries, buf_a, buf_b, buf_w)


def reduce_kernel(count, sums_ref, out_ref, held, slots, send_sem, recv_sem):
    x = lax.axis_index("dp_0")
    zl = lax.axis_index("dp_1")
    zh = lax.axis_index("fsdp_0")
    y = lax.axis_index("fsdp_1")
    c = lax.axis_index("fsdp_2")
    mine = (zh * 2 + zl, y, x * 2 + c)

    def peer(stage, step):
        other = lax.rem(mine[stage] + step, 8)
        if stage == 0:
            return other, {"fsdp_0": other // 2, "dp_1": lax.rem(other, 2)}
        if stage == 1:
            return other, {"fsdp_1": other}
        return other, {"dp_0": other // 2, "fsdp_2": lax.rem(other, 2)}

    barrier = pltpu.get_barrier_semaphore()
    for stage in range(3):
        for step in range(1, 8):
            pl.semaphore_signal(
                barrier, inc=1, device_id=peer(stage, step)[1], device_id_type=MESH
            )
    rows = jnp.sum(jnp.sum(sums_ref[...], axis=1), axis=1, keepdims=True)
    line = lax.broadcasted_iota(jnp.int32, (HEADS, HD), 0)
    lane = lax.broadcasted_iota(jnp.int32, (HEADS, HD), 1)
    total = jnp.broadcast_to(
        jnp.sum(jnp.where(line == lane, rows, 0.0), axis=0, keepdims=True), (8, HD)
    )
    pl.semaphore_wait(barrier, 21)
    for stage in range(3):
        held[stage] = total
        slots[stage, mine[stage]] = total
        copies = []
        for step in range(1, 8):
            other, where = peer(stage, step)
            copy = pltpu.make_async_remote_copy(
                src_ref=held.at[stage],
                dst_ref=slots.at[stage, mine[stage]],
                send_sem=send_sem.at[stage, step],
                recv_sem=recv_sem.at[stage, mine[stage]],
                device_id=where,
                device_id_type=MESH,
            )
            copy.start()
            copies.append(copy)
        for step in range(1, 8):
            other, where = peer(stage, step)
            pltpu.make_async_remote_copy(
                src_ref=held.at[stage],
                dst_ref=slots.at[stage, other],
                send_sem=send_sem.at[stage, step],
                recv_sem=recv_sem.at[stage, other],
                device_id=where,
                device_id_type=MESH,
            ).wait_recv()
        total = jnp.sum(slots[stage], axis=0)
        for copy in copies:
            copy.wait_send()
    out_ref[...] = total / count


def reduce_all(sums, count):
    vmem = pl.BlockSpec(memory_space=pltpu.VMEM)
    return pl.pallas_call(
        functools.partial(reduce_kernel, count),
        out_shape=jax.ShapeDtypeStruct((8, HD), jnp.float32),
        in_specs=[vmem],
        out_specs=vmem,
        scratch_shapes=[
            pltpu.VMEM((3, 8, HD), jnp.float32),
            pltpu.VMEM((3, 8, 8, HD), jnp.float32),
            pltpu.SemaphoreType.DMA((3, 8)),
            pltpu.SemaphoreType.DMA((3, 8)),
        ],
        compiler_params=pltpu.CompilerParams(collective_id=1, has_side_effects=True),
        name="reduce",
    )(sums)


def body(tokens, queries, key_weight, value_weight, key_variance, sign_bits):
    buf_a, buf_b, buf_w = gather(key_weight, value_weight, key_variance, sign_bits)
    attended, spread, sums = attend(tokens[0], queries[0], buf_a, buf_b, buf_w)
    count = lax.axis_size(ALL) * LEN * HD
    mean = reduce_all(sums, float(count))
    return attended[None], spread[None], mean[0, :HEADS]


def solution(mesh):
    torus = Mesh(mesh.devices.reshape(4, 2, 4, 8, 2), ALL)
    placed = (P(ALL, None, None), P(ALL, None, None)) + (P(FSDP, None),) * 4
    return jax.shard_map(
        body,
        mesh=torus,
        in_specs=placed,
        out_specs=(P(ALL, None, None), P(ALL, None, None), P()),
        check_vma=False,
    )
```
